32 devices in a mesh: station: 4 (over z), cores: 8 (over y, x, core).
Axes of the slice: x: 2, y: 2, z: 4, core: 2. Of those that a mesh axis runs over, the one named last changes fastest.
Arguments:
- samples: bfloat16 [2, 64, 1048576], P(None, 'station', 'cores'), may hold values from -6 to 6
- delays: int32 [64], P('station'), may hold values from 0 to 32768, as said below
- fringe_rate: int32 [64], P('station'), may hold values from 0 to 4095
- station_of_row: int32 [64], replicated, may hold values from 0 to 63, each once
Outputs:
- visibilities: float32 [65536, 4096], P(('station', 'cores'))
The draws below stay inside these ranges and needn't reach their ends.
Inputs may be any that keep to these rules, and one draw needn't show every extreme that they name: `delays`: every delay lies between 0 and 32768, and some station's delay is exactly 32768. `station_of_row`: each station number appears once.
All inputs are finite; a program needn't handle non-finite values.
Results may differ from the reference program's by a relative error of at most 0.0035.
Values may be sent and summed in bfloat16 or wider, within the bound.
A program may use at most 640 MiB of HBM per device.

```python
import math
import jax
import jax.numpy as jnp
from jax import lax

S = 64
NCH = 65536
SEGS = 16
TIME = 1048576
MAXD = 32768
PERIOD = 262144


def draw_delays(key, part):
    first, second = jax.random.split(jax.random.fold_in(key, 17))
    values = jax.random.randint(first, (S,), 0, MAXD + 1)
    where = jax.random.randint(second, (), 0, S)
    return values.at[where].set(MAXD).astype(jnp.int32)


def set_ends(array, rng, low, largest):
    longest = array.shape.index(max(array.shape))
    spots = []
    for shift in (0, 1):
        where = [jax.random.randint(jax.random.fold_in(rng, axis), (), 0, length) for axis, length in enumerate(array.shape)]
        where[longest] = (where[longest] + shift) % array.shape[longest]
        spots.append(tuple(where))
    return array.at[spots[0]].set(low).at[spots[1]].set(largest)


def block_levels(own_key, dims, pieces, least, high):
    gain = 1.0
    for position, blocks in pieces:
        heights = jax.random.uniform(jax.random.fold_in(jax.random.fold_in(own_key, 6), position), (blocks,), jnp.float32, least / len(pieces), high / len(pieces))
        gain = gain * jnp.repeat(jnp.exp(heights), dims[position] // blocks).reshape((-1,) + (1,) * (len(dims) - 1 - position))
    return gain


def noise(key, extent, deviation, reach, cuts=(), kind=jnp.bfloat16):
    entries = jax.random.normal(key, extent, jnp.float32) * deviation
    if len(cuts) > 0:
        entries = block_levels(key, extent, cuts, -0.22, 0.18) * entries
    return jnp.clip(entries, min=-reach, max=reach).astype(kind)


def setup_inputs(seed: int = 0) -> dict:
    splits = jax.random.split(jax.random.key(seed), 5)
    samples = noise(splits[0], (2, S, TIME), 1.0, 6.0, ((1, 4), (2, 8)))
    delays = draw_delays(jax.random.fold_in(splits[4], 71), 0)
    fringe_rate = set_ends(jax.random.randint(splits[2], (S,), 0, 4096), jax.random.fold_in(splits[2], 1), 0, 4095).astype(jnp.int32)
    station_of_row = jax.random.permutation(splits[3], S).astype(jnp.int32)
    return dict(samples=samples, delays=delays, fringe_rate=fringe_rate, station_of_row=station_of_row)


def station_spectrum(row, delay, rate):
    padded = jnp.pad(row, ((0, 0), (0, MAXD)))
    aligned = lax.dynamic_slice_in_dim(padded, delay, TIME, axis=1).astype(jnp.float32)
    moment = jnp.arange(TIME, dtype=jnp.int32) % PERIOD
    counter = (rate * moment) % PERIOD
    angle = counter.astype(jnp.float32) * (2.0 * math.pi / PERIOD)
    cosine = jnp.cos(angle)
    sine = jnp.sin(angle)
    real_part = aligned[0] * cosine + aligned[1] * sine
    imag_part = aligned[1] * cosine - aligned[0] * sine
    signal = (real_part + 1j * imag_part).reshape(SEGS, NCH)
    spectrum = jnp.fft.fft(signal, axis=-1, norm="ortho")
    return jnp.stack([jnp.real(spectrum), jnp.imag(spectrum)]).astype(jnp.bfloat16)


def reference(samples, delays, fringe_rate, station_of_row):
    rows = jnp.moveaxis(samples, 1, 0)
    spectra = lax.map(lambda item: station_spectrum(item[0], item[1], item[2]), (rows, delays, fringe_rate))
    spectra = jnp.moveaxis(spectra, 0, 1)
    inverse = jnp.argsort(station_of_row).astype(jnp.int32)
    ordered = jnp.take(spectra, inverse, axis=1)
    width = NCH // 16
    blocks = jnp.moveaxis(ordered.reshape(2, S, SEGS, 16, width), 3, 0)
    upper = jnp.arange(S)[:, None] <= jnp.arange(S)[None, :]

    def block_visibility(block):
        real_in = block[0].astype(jnp.float32)
        imag_in = block[1].astype(jnp.float32)
        real_out = jnp.einsum("sgc,tgc->cst", real_in, real_in) + jnp.einsum("sgc,tgc->cst", imag_in, imag_in)
        imag_out = jnp.einsum("sgc,tgc->cst", imag_in, real_in) - jnp.einsum("sgc,tgc->cst", real_in, imag_in)
        packed = jnp.where(upper[None], real_out, imag_out) * (1.0 / SEGS)
        return packed.reshape(width, S * S)

    result = lax.map(block_visibility, blocks)
    return result.reshape(NCH, S * S)
```

```python
import functools
import math

import jax
import jax.numpy as jnp
import numpy as np
from jax import lax
from jax.experimental import pallas as pl
from jax.experimental.pallas import tpu as pltpu
from jax.sharding import PartitionSpec as P

S = 64
NCH = 65536
ROOT = 256
MAXD = 32768
PERIOD = 262144
F32 = jnp.float32
BF16 = jnp.bfloat16


def passed_along(x, axis, by):
    count = lax.axis_size(axis)
    pairs = [(i, i + by) for i in range(count) if 0 <= i + by < count]
    return lax.ppermute(x, axis, pairs)


def dft_table(length, scale):
    index = np.arange(ROOT)
    angle = (index[:, None] * index[None, :] % length) * (2.0 * math.pi / length)
    return np.stack([np.cos(angle) * scale, -np.sin(angle) * scale]).astype(np.float32)


def halves(x):
    high = x.astype(BF16)
    return high, (x - high.astype(F32)).astype(BF16)


def block_form(real, imag):
    return jnp.concatenate(
        [jnp.concatenate([real, -imag], axis=1), jnp.concatenate([imag, real], axis=1)], axis=0
    )


def dot(a, b, dims=((1,), (0,))):
    return lax.dot_general(a, b, (dims, ((), ())), preferred_element_type=F32)


def phases(counter):
    angle = (counter % PERIOD).astype(F32) * (2.0 * math.pi / PERIOD)
    return jnp.stack([jnp.cos(angle), -jnp.sin(angle)], axis=-2)


def front_kernel(segs, delays, x_ref, follow_ref, u_ref, v_ref, f_ref, tw_ref, gh_ref, gl_ref, o_ref, ext):
    r = pl.program_id(0)
    here = x_ref.shape[2]
    after = follow_ref.shape[2]
    for p in range(2):
        for h in range(2):
            cols = slice(h * 128, h * 128 + 128)
            ext[p, h, :here] = x_ref[p, 0, :, cols].astype(F32)
            ext[p, h, here : here + after] = follow_ref[p, 0, :, cols].astype(F32)
    delay = delays[r]
    down = delay // ROOT
    across = delay % ROOT
    u_real, u_imag = u_ref[0, 0:1], u_ref[0, 1:2]
    f_real, f_imag = f_ref[0], f_ref[1]
    fh_real, fl_real = halves(f_real * u_real - f_imag * u_imag)
    fh_imag, fl_imag = halves(f_real * u_imag + f_imag * u_real)
    f_high = block_form(fh_real, fh_imag)
    f_low = block_form(fl_real, fl_imag)
    lane = lax.broadcasted_iota(jnp.int32, (ROOT, ROOT), 1)
    kept = lane >= across
    for s in range(segs):
        parts = []
        for p in range(2):
            begin = down + s * ROOT
            first = jnp.concatenate([ext[p, h, pl.ds(begin, ROOT), :] for h in range(2)], axis=1)
            second = jnp.concatenate([ext[p, h, pl.ds(begin + 1, ROOT), :] for h in range(2)], axis=1)
            parts.append(pltpu.roll(jnp.where(kept, first, second), ROOT - across, 1).astype(BF16))
        x = jnp.concatenate(parts, axis=0)
        y = dot(f_high, x) + dot(f_low, x)
        y_real, y_imag = y[:ROOT], y[ROOT:]
        v_real, v_imag = v_ref[0, s, 0:1], v_ref[0, s, 1:2]
        t_real = tw_ref[0] * v_real - tw_ref[1] * v_imag
        t_imag = tw_ref[0] * v_imag + tw_ref[1] * v_real
        mh_real, ml_real = halves(y_real * t_real - y_imag * t_imag)
        mh_imag, ml_imag = halves(y_real * t_imag + y_imag * t_real)
        high = jnp.concatenate([mh_real, mh_imag], axis=1)
        low = jnp.concatenate([ml_real, ml_imag], axis=1)
        rows = ((1,), (1,))
        z = dot(gh_ref[...], high, rows) + dot(gh_ref[...], low, rows) + dot(gl_ref[...], high, rows)
        z = z.astype(BF16)
        for p in range(2):
            o_ref[:, p, s, 0] = z[p * ROOT : (p + 1) * ROOT].reshape(o_ref.shape[0], o_ref.shape[4], ROOT)


def front(samples, following, delays, u, v, owners):
    _, local_rows, here, _ = samples.shape
    after = following.shape[2]
    segs = here // ROOT
    owned = ROOT // owners
    table = dft_table(ROOT, 1.0)
    gh, gl = halves(block_form(jnp.asarray(table[0]), jnp.asarray(table[1])))
    whole3 = pl.BlockSpec((2, ROOT, ROOT), lambda r, d: (0, 0, 0))
    whole2 = pl.BlockSpec((2 * ROOT, 2 * ROOT), lambda r, d: (0, 0))
    return pl.pallas_call(
        functools.partial(front_kernel, segs),
        grid_spec=pltpu.PrefetchScalarGridSpec(
            num_scalar_prefetch=1,
            grid=(local_rows,),
            in_specs=[
                pl.BlockSpec((2, 1, here, ROOT), lambda r, d: (0, r, 0, 0)),
                pl.BlockSpec((2, 1, after, ROOT), lambda r, d: (0, r, 0, 0)),
                pl.BlockSpec((1, 2, ROOT), lambda r, d: (r, 0, 0)),
                pl.BlockSpec((1, segs, 2, ROOT), lambda r, d: (r, 0, 0, 0)),
                whole3,
                whole3,
                whole2,
                whole2,
            ],
            out_specs=pl.BlockSpec((owners, 2, segs, 1, owned, ROOT), lambda r, d: (0, 0, 0, r, 0, 0)),
            scratch_shapes=[
                pltpu.VMEM((2, 2, here + after + 8, 128), F32),
            ],
        ),
        out_shape=jax.ShapeDtypeStruct((owners, 2, segs, local_rows, owned, ROOT), BF16),
        compiler_params=pltpu.CompilerParams(vmem_limit_bytes=56 * 1024 * 1024),
        name="front",
    )(delays, samples, following, u, v, jnp.asarray(table), jnp.asarray(dft_table(NCH, 1.0 / 256.0)), gh, gl)


def cross_kernel(total_segs, x_ref, sel_ref, o_ref, wide, packed):
    for g in range(total_segs):
        t = dot(x_ref[0, g], sel_ref[...], ((0,), (0,)))
        wide[pl.ds(2 * g * ROOT, ROOT), :] = t[:, :128]
        wide[pl.ds((2 * g + 1) * ROOT, ROOT), :] = t[:, 128:]
    a = lax.broadcasted_iota(jnp.int32, (S, 128), 0)
    lane = lax.broadcasted_iota(jnp.int32, (S, 128), 1)
    straight = jnp.where(lane < S, lane - a, a - lane + S - 1) >= 0
    left = lax.broadcasted_iota(jnp.int32, (8, 128), 1) < S

    @pl.loop(0, ROOT // 8)
    def _(block):
        for c in range(8):
            w = wide[pl.ds(block * 8 + c, 2 * total_segs, stride=ROOT), :].astype(BF16)
            out = dot(w[:, :S], w, ((0,), (0,))) * (1.0 / total_segs)
            packed[c * S : (c + 1) * S, :] = jnp.where(straight, out, pltpu.roll(out, S, 1))
        for j in range(S // 2):
            even = packed[pl.ds(2 * j, 8, stride=S), :]
            odd = packed[pl.ds(2 * j + 1, 8, stride=S), :]
            o_ref[pl.ds(pl.multiple_of(block * 8, 8), 8), j * 128 : (j + 1) * 128] = jnp.where(left, even, odd)


def cross(x, sel):
    owned, total_segs = x.shape[0], x.shape[1]
    return pl.pallas_call(
        functools.partial(cross_kernel, total_segs),
        grid=(owned,),
        in_specs=[
            pl.BlockSpec((1, total_segs, 2 * S, ROOT), lambda q: (q, 0, 0, 0)),
            pl.BlockSpec((2 * S, 4 * S), lambda q: (0, 0)),
        ],
        out_specs=pl.BlockSpec((ROOT, S * S), lambda q: (q, 0)),
        out_shape=jax.ShapeDtypeStruct((owned * ROOT, S * S), F32),
        scratch_shapes=[
            pltpu.VMEM((2 * total_segs * ROOT, 128), F32),
            pltpu.VMEM((8 * S, 128), F32),
        ],
        compiler_params=pltpu.CompilerParams(vmem_limit_bytes=56 * 1024 * 1024),
        name="cross",
    )(x, sel)


def shards(samples, delays, fringe_rate, station_of_row):
    _, local_rows, local_time = samples.shape
    segs = local_time // NCH
    groups = lax.axis_size("station")
    blocks = lax.axis_size("cores")
    owners = groups * blocks
    head = samples[:, :, :MAXD].reshape(2, local_rows, MAXD // ROOT, ROOT)
    following = passed_along(head, "cores", -1)
    shaped = samples.reshape(2, local_rows, local_time // ROOT, ROOT)
    index = jnp.arange(ROOT, dtype=jnp.int32)
    u = phases(fringe_rate[:, None] * (ROOT * index)[None, :])
    start = (lax.axis_index("cores") * segs + jnp.arange(segs, dtype=jnp.int32)) * NCH % PERIOD
    v = phases(fringe_rate[:, None, None] * (start[:, None] + index[None, :])[None])
    spectra = front(shaped, following, delays, u, v, owners)
    arrived = lax.all_to_all(spectra, ("station", "cores"), split_axis=0, concat_axis=0, tiled=True)
    owned = arrived.shape[4]
    arrived = arrived.reshape(groups, blocks, 2, segs, local_rows, owned, ROOT)
    ordered = arrived.transpose(5, 1, 3, 2, 0, 4, 6).reshape(owned, blocks * segs, 2 * S, ROOT)
    pick = (station_of_row[:, None] == jnp.arange(S, dtype=jnp.int32)[None, :]).astype(BF16)
    none = jnp.zeros_like(pick)
    sel = jnp.concatenate(
        [
            jnp.concatenate([pick, none, none, pick], axis=1),
            jnp.concatenate([none, -pick, pick, none], axis=1),
        ],
        axis=0,
    )
    return cross(ordered, sel)


def solution(mesh):
    in_specs = (P(None, "station", "cores"), P("station"), P("station"), P())
    out_specs = P(("station", "cores"), None)
    return jax.shard_map(shards, mesh=mesh, in_specs=in_specs, out_specs=out_specs, check_vma=False)
```

```python
import functools
import math

import jax
import jax.numpy as jnp
import numpy as np
from jax import lax
from jax.experimental import pallas as pl
from jax.experimental.pallas import tpu as pltpu
from jax.sharding import PartitionSpec as P

S = 64
NCH = 65536
ROOT = 256
MAXD = 32768
PERIOD = 262144
F32 = jnp.float32
BF16 = jnp.bfloat16


def passed_along(x, axis, by):
    count = lax.axis_size(axis)
    pairs = [(i, i + by) for i in range(count) if 0 <= i + by < count]
    return lax.ppermute(x, axis, pairs)


def dft_table(length, scale):
    index = np.arange(ROOT)
    angle = (index[:, None] * index[None, :] % length) * (2.0 * math.pi / length)
    return np.stack([np.cos(angle) * scale, -np.sin(angle) * scale]).astype(np.float32)


def halves(x):
    high = x.astype(BF16)
    return high, (x - high.astype(F32)).astype(BF16)


def block_form(real, imag):
    return jnp.concatenate(
        [jnp.concatenate([real, -imag], axis=1), jnp.concatenate([imag, real], axis=1)], axis=0
    )


def dot(a, b, dims=((1,), (0,))):
    return lax.dot_general(a, b, (dims, ((), ())), preferred_element_type=F32)


def phases(counter):
    angle = (counter % PERIOD).astype(F32) * (2.0 * math.pi / PERIOD)
    return jnp.stack([jnp.cos(angle), -jnp.sin(angle)], axis=-2)


def front_kernel(segs, delays, x_ref, follow_ref, u_ref, v_ref, f_ref, tw_ref, gh_ref, gl_ref, o_ref, ext):
    r = pl.program_id(0)
    here = x_ref.shape[2]
    after = follow_ref.shape[2]
    for p in range(2):
        for h in range(2):
            cols = slice(h * 128, h * 128 + 128)
            ext[p, h, :here] = x_ref[p, 0, :, cols].astype(F32)
            ext[p, h, here : here + after] = follow_ref[p, 0, :, cols].astype(F32)
    delay = delays[r]
    down = delay // ROOT
    across = delay % ROOT
    u_real, u_imag = u_ref[0, 0:1], u_ref[0, 1:2]
    f_real, f_imag = f_ref[0], f_ref[1]
    fh_real, fl_real = halves(f_real * u_real - f_imag * u_imag)
    fh_imag, fl_imag = halves(f_real * u_imag + f_imag * u_real)
    f_high = block_form(fh_real, fh_imag)
    f_low = block_form(fl_real, fl_imag)
    lane = lax.broadcasted_iota(jnp.int32, (ROOT, ROOT), 1)
    kept = lane >= across
    for s in range(segs):
        parts = []
        for p in range(2):
            begin = down + s * ROOT
            first = jnp.concatenate([ext[p, h, pl.ds(begin, ROOT), :] for h in range(2)], axis=1)
            second = jnp.concatenate([ext[p, h, pl.ds(begin + 1, ROOT), :] for h in range(2)], axis=1)
            parts.append(pltpu.roll(jnp.where(kept, first, second), ROOT - across, 1).astype(BF16))
        x = jnp.concatenate(parts, axis=0)
        y = dot(f_high, x) + dot(f_low, x)
        y_real, y_imag = y[:ROOT], y[ROOT:]
        v_real, v_imag = v_ref[0, s, 0:1], v_ref[0, s, 1:2]
        t_real = tw_ref[0] * v_real - tw_ref[1] * v_imag
        t_imag = tw_ref[0] * v_imag + tw_ref[1] * v_real
        mh_real, ml_real = halves(y_real * t_real - y_imag * t_imag)
        mh_imag, ml_imag = halves(y_real * t_imag + y_imag * t_real)
        high = jnp.concatenate([mh_real, mh_imag], axis=1)
        low = jnp.concatenate([ml_real, ml_imag], axis=1)
        rows = ((1,), (1,))
        z = dot(gh_ref[...], high, rows) + dot(gh_ref[...], low, rows) + dot(gl_ref[...], high, rows)
        z = z.astype(BF16)
        for p in range(2):
            o_ref[:, p, s, 0] = z[p * ROOT : (p + 1) * ROOT].reshape(o_ref.shape[0], o_ref.shape[4], ROOT)


def front(samples, following, delays, u, v, owners):
    _, local_rows, here, _ = samples.shape
    after = following.shape[2]
    segs = here // ROOT
    owned = ROOT // owners
    table = dft_table(ROOT, 1.0)
    gh, gl = halves(block_form(jnp.asarray(table[0]), jnp.asarray(table[1])))
    whole3 = pl.BlockSpec((2, ROOT, ROOT), lambda r, d: (0, 0, 0))
    whole2 = pl.BlockSpec((2 * ROOT, 2 * ROOT), lambda r, d: (0, 0))
    return pl.pallas_call(
        functools.partial(front_kernel, segs),
        grid_spec=pltpu.PrefetchScalarGridSpec(
            num_scalar_prefetch=1,
            grid=(local_rows,),
            in_specs=[
                pl.BlockSpec((2, 1, here, ROOT), lambda r, d: (0, r, 0, 0)),
                pl.BlockSpec((2, 1, after, ROOT), lambda r, d: (0, r, 0, 0)),
                pl.BlockSpec((1, 2, ROOT), lambda r, d: (r, 0, 0)),
                pl.BlockSpec((1, segs, 2, ROOT), lambda r, d: (r, 0, 0, 0)),
                whole3,
                whole3,
                whole2,
                whole2,
            ],
            out_specs=pl.BlockSpec((owners, 2, segs, 1, owned, ROOT), lambda r, d: (0, 0, 0, r, 0, 0)),
            scratch_shapes=[
                pltpu.VMEM((2, 2, here + after + 8, 128), F32),
            ],
        ),
        out_shape=jax.ShapeDtypeStruct((owners, 2, segs, local_rows, owned, ROOT), BF16),
        compiler_params=pltpu.CompilerParams(vmem_limit_bytes=56 * 1024 * 1024),
        name="front",
    )(delays, samples, following, u, v, jnp.asarray(table), jnp.asarray(dft_table(NCH, 1.0 / 256.0)), gh, gl)


def cross_kernel(groups, blocks, segs, local_rows, x_ref, sel_ref, o_ref, recv, wide, packed, send_sem, recv_sem, own_sem):
    q = pl.program_id(0)
    count = pl.num_programs(0)
    owners = groups * blocks
    total_segs = blocks * segs
    me = lax.axis_index("station") * blocks + lax.axis_index("cores")

    def coords(d):
        return {"station": d // blocks, "cores": lax.rem(d, blocks)}

    def remote(step, i):
        dest = lax.rem(me + i, owners)
        return pltpu.make_async_remote_copy(
            src_ref=x_ref.at[step, dest],
            dst_ref=recv.at[step, me],
            send_sem=send_sem.at[step],
            recv_sem=recv_sem.at[step],
            device_id=coords(dest),
            device_id_type=pl.DeviceIdType.MESH,
        )

    def own(step):
        return pltpu.make_async_copy(x_ref.at[step, me], recv.at[step, me], own_sem.at[step])

    @pl.when(q == 0)
    def _():
        barrier = pltpu.get_barrier_semaphore()

        @pl.loop(1, owners)
        def _(i):
            pl.semaphore_signal(
                barrier, inc=1, device_id=coords(lax.rem(me + i, owners)), device_id_type=pl.DeviceIdType.MESH
            )

        pl.semaphore_wait(barrier, owners - 1)

        @pl.loop(0, x_ref.shape[0])
        def _(step):
            own(step).start()

            @pl.loop(1, owners)
            def _(i):
                remote(step, i).start()

    own(q).wait()

    others = recv.at[q, pl.ds(0, owners - 1)]
    pltpu.make_async_copy(others, others, recv_sem.at[q]).wait()

    @pl.when(q == count - 1)
    def _():
        @pl.loop(0, x_ref.shape[0])
        def _(step):
            gone = recv.at[step, pl.ds(0, owners - 1)]
            pltpu.make_async_copy(gone, gone, send_sem.at[step]).wait()

    for g in range(total_segs):
        c, s = g // segs, g % segs
        x = jnp.concatenate(
            [
                recv[q, st * blocks + c, (p * segs + s) * local_rows : (p * segs + s + 1) * local_rows, :]
                for p in range(2)
                for st in range(groups)
            ],
            axis=0,
        )
        t = dot(x, sel_ref[...], ((0,), (0,)))
        wide[pl.ds(2 * g * ROOT, ROOT), :] = t[:, :128]
        wide[pl.ds((2 * g + 1) * ROOT, ROOT), :] = t[:, 128:]
    a = lax.broadcasted_iota(jnp.int32, (S, 128), 0)
    lane = lax.broadcasted_iota(jnp.int32, (S, 128), 1)
    straight = jnp.where(lane < S, lane - a, a - lane + S - 1) >= 0
    left = lax.broadcasted_iota(jnp.int32, (8, 128), 1) < S

    @pl.loop(0, ROOT // 8)
    def _(block):
        for c in range(8):
            w = wide[pl.ds(block * 8 + c, 2 * total_segs, stride=ROOT), :].astype(BF16)
            out = dot(w[:, :S], w, ((0,), (0,))) * (1.0 / total_segs)
            packed[c * S : (c + 1) * S, :] = jnp.where(straight, out, pltpu.roll(out, S, 1))
        for j in range(S // 2):
            even = packed[pl.ds(2 * j, 8, stride=S), :]
            odd = packed[pl.ds(2 * j + 1, 8, stride=S), :]
            o_ref[pl.ds(pl.multiple_of(block * 8, 8), 8), j * 128 : (j + 1) * 128] = jnp.where(left, even, odd)


def cross(x, sel, groups, blocks, segs, local_rows):
    owned = x.shape[0]
    total_segs = blocks * segs
    return pl.pallas_call(
        functools.partial(cross_kernel, groups, blocks, segs, local_rows),
        grid=(owned,),
        in_specs=[
            pl.BlockSpec(memory_space=pl.ANY),
            pl.BlockSpec((2 * S, 4 * S), lambda q: (0, 0)),
        ],
        out_specs=pl.BlockSpec((ROOT, S * S), lambda q: (q, 0)),
        out_shape=jax.ShapeDtypeStruct((owned * ROOT, S * S), F32),
        scratch_shapes=[
            pltpu.VMEM(x.shape, BF16),
            pltpu.VMEM((2 * total_segs * ROOT, 128), F32),
            pltpu.VMEM((8 * S, 128), F32),
            pltpu.SemaphoreType.DMA((owned,)),
            pltpu.SemaphoreType.DMA((owned,)),
            pltpu.SemaphoreType.DMA((owned,)),
        ],
        compiler_params=pltpu.CompilerParams(
            vmem_limit_bytes=48 * 1024 * 1024, collective_id=0, has_side_effects=True
        ),
        name="cross",
    )(x, sel)


def shards(samples, delays, fringe_rate, station_of_row):
    _, local_rows, local_time = samples.shape
    segs = local_time // NCH
    groups = lax.axis_size("station")
    blocks = lax.axis_size("cores")
    owners = groups * blocks
    head = samples[:, :, :MAXD].reshape(2, local_rows, MAXD // ROOT, ROOT)
    following = passed_along(head, "cores", -1)
    shaped = samples.reshape(2, local_rows, local_time // ROOT, ROOT)
    index = jnp.arange(ROOT, dtype=jnp.int32)
    u = phases(fringe_rate[:, None] * (ROOT * index)[None, :])
    start = (lax.axis_index("cores") * segs + jnp.arange(segs, dtype=jnp.int32)) * NCH % PERIOD
    v = phases(fringe_rate[:, None, None] * (start[:, None] + index[None, :])[None])
    spectra = front(shaped, following, delays, u, v, owners)
    owned = spectra.shape[4]
    sent = spectra.transpose(4, 0, 1, 2, 3, 5).reshape(owned, owners, 2 * segs * local_rows, ROOT)
    pick = (station_of_row[:, None] == jnp.arange(S, dtype=jnp.int32)[None, :]).astype(BF16)
    none = jnp.zeros_like(pick)
    sel = jnp.concatenate(
        [
            jnp.concatenate([pick, none, none, pick], axis=1),
            jnp.concatenate([none, -pick, pick, none], axis=1),
        ],
        axis=0,
    )
    return cross(sent, sel, groups, blocks, segs, local_rows)


def solution(mesh):
    in_specs = (P(None, "station", "cores"), P("station"), P("station"), P())
    out_specs = P(("station", "cores"), None)
    return jax.shard_map(shards, mesh=mesh, in_specs=in_specs, out_specs=out_specs, check_vma=False)
```

```python
import functools
import math

import jax
import jax.numpy as jnp
import numpy as np
from jax import lax
from jax.experimental import pallas as pl
from jax.experimental.pallas import tpu as pltpu
from jax.sharding import PartitionSpec as P

S = 64
NCH = 65536
ROOT = 256
MAXD = 32768
PERIOD = 262144
F32 = jnp.float32
BF16 = jnp.bfloat16


def passed_along(x, axis, by):
    count = lax.axis_size(axis)
    pairs = [(i, i + by) for i in range(count) if 0 <= i + by < count]
    return lax.ppermute(x, axis, pairs)


def dft_table(length, scale):
    index = np.arange(ROOT)
    angle = (index[:, None] * index[None, :] % length) * (2.0 * math.pi / length)
    return np.stack([np.cos(angle) * scale, -np.sin(angle) * scale]).astype(np.float32)


def halves(x):
    high = x.astype(BF16)
    return high, (x - high.astype(F32)).astype(BF16)


def block_form(real, imag):
    return jnp.concatenate(
        [jnp.concatenate([real, -imag], axis=1), jnp.concatenate([imag, real], axis=1)], axis=0
    )


def dot(a, b, dims=((1,), (0,))):
    return lax.dot_general(a, b, (dims, ((), ())), preferred_element_type=F32)


def phases(counter):
    angle = (counter % PERIOD).astype(F32) * (2.0 * math.pi / PERIOD)
    return jnp.stack([jnp.cos(angle), -jnp.sin(angle)], axis=-2)


def front_kernel(segs, delays, x_ref, follow_ref, u_ref, v_ref, f_ref, tw_ref, gh_ref, gl_ref, o_ref, ext):
    r = pl.program_id(0)
    here = x_ref.shape[2]
    after = follow_ref.shape[2]
    for p in range(2):
        for h in range(2):
            cols = slice(h * 128, h * 128 + 128)
            ext[p, h, :here] = x_ref[p, 0, :, cols].astype(F32)
            ext[p, h, here : here + after] = follow_ref[p, 0, :, cols].astype(F32)
    delay = delays[r]
    down = delay // ROOT
    across = delay % ROOT
    u_real, u_imag = u_ref[0, 0:1], u_ref[0, 1:2]
    f_real, f_imag = f_ref[0], f_ref[1]
    fh_real, fl_real = halves(f_real * u_real - f_imag * u_imag)
    fh_imag, fl_imag = halves(f_real * u_imag + f_imag * u_real)
    f_high = block_form(fh_real, fh_imag)
    f_low = block_form(fl_real, fl_imag)
    lane = lax.broadcasted_iota(jnp.int32, (ROOT, ROOT), 1)
    kept = lane >= across
    for s in range(segs):
        parts = []
        for p in range(2):
            begin = down + s * ROOT
            first = jnp.concatenate([ext[p, h, pl.ds(begin, ROOT), :] for h in range(2)], axis=1)
            second = jnp.concatenate([ext[p, h, pl.ds(begin + 1, ROOT), :] for h in range(2)], axis=1)
            parts.append(pltpu.roll(jnp.where(kept, first, second), ROOT - across, 1).astype(BF16))
        x = jnp.concatenate(parts, axis=0)
        y = dot(f_high, x) + dot(f_low, x)
        y_real, y_imag = y[:ROOT], y[ROOT:]
        v_real, v_imag = v_ref[0, s, 0:1], v_ref[0, s, 1:2]
        t_real = tw_ref[0] * v_real - tw_ref[1] * v_imag
        t_imag = tw_ref[0] * v_imag + tw_ref[1] * v_real
        mh_real, ml_real = halves(y_real * t_real - y_imag * t_imag)
        mh_imag, ml_imag = halves(y_real * t_imag + y_imag * t_real)
        high = jnp.concatenate([mh_real, mh_imag], axis=1)
        low = jnp.concatenate([ml_real, ml_imag], axis=1)
        rows = ((1,), (1,))
        z = dot(gh_ref[...], high, rows) + dot(gh_ref[...], low, rows) + dot(gl_ref[...], high, rows)
        z = z.astype(BF16)
        for p in range(2):
            o_ref[:, p, s, 0] = z[p * ROOT : (p + 1) * ROOT].reshape(o_ref.shape[0], o_ref.shape[4], ROOT)


def front(samples, following, delays, u, v, owners):
    _, local_rows, here, _ = samples.shape
    after = following.shape[2]
    segs = here // ROOT
    owned = ROOT // owners
    table = dft_table(ROOT, 1.0)
    gh, gl = halves(block_form(jnp.asarray(table[0]), jnp.asarray(table[1])))
    whole3 = pl.BlockSpec((2, ROOT, ROOT), lambda r, d: (0, 0, 0))
    whole2 = pl.BlockSpec((2 * ROOT, 2 * ROOT), lambda r, d: (0, 0))
    return pl.pallas_call(
        functools.partial(front_kernel, segs),
        grid_spec=pltpu.PrefetchScalarGridSpec(
            num_scalar_prefetch=1,
            grid=(local_rows,),
            in_specs=[
                pl.BlockSpec((2, 1, here, ROOT), lambda r, d: (0, r, 0, 0)),
                pl.BlockSpec((2, 1, after, ROOT), lambda r, d: (0, r, 0, 0)),
                pl.BlockSpec((1, 2, ROOT), lambda r, d: (r, 0, 0)),
                pl.BlockSpec((1, segs, 2, ROOT), lambda r, d: (r, 0, 0, 0)),
                whole3,
                whole3,
                whole2,
                whole2,
            ],
            out_specs=pl.BlockSpec((owners, 2, segs, 1, owned, ROOT), lambda r, d: (0, 0, 0, r, 0, 0)),
            scratch_shapes=[
                pltpu.VMEM((2, 2, here + after + 8, 128), F32),
            ],
        ),
        out_shape=jax.ShapeDtypeStruct((owners, 2, segs, local_rows, owned, ROOT), BF16),
        compiler_params=pltpu.CompilerParams(vmem_limit_bytes=56 * 1024 * 1024),
        name="front",
    )(delays, samples, following, u, v, jnp.asarray(table), jnp.asarray(dft_table(NCH, 1.0 / 256.0)), gh, gl)


def cross_kernel(groups, blocks, segs, local_rows, x_ref, sel_ref, o_ref, recv, wide, packed, send_sem, recv_sem, own_sem):
    q = pl.program_id(0)
    count = pl.num_programs(0)
    owners = groups * blocks
    total_segs = blocks * segs
    me = lax.axis_index("station") * blocks + lax.axis_index("cores")

    def coords(d):
        return {"station": d // blocks, "cores": lax.rem(d, blocks)}

    def remote(step, i):
        dest = lax.rem(me + lax.rem(i, groups) * blocks + i // groups, owners)
        return pltpu.make_async_remote_copy(
            src_ref=x_ref.at[step, dest],
            dst_ref=recv.at[step, me],
            send_sem=send_sem.at[step],
            recv_sem=recv_sem.at[step],
            device_id=coords(dest),
            device_id_type=pl.DeviceIdType.MESH,
        )

    def own(step):
        return pltpu.make_async_copy(x_ref.at[step, me], recv.at[step, me], own_sem.at[step])

    @pl.when(q == 0)
    def _():
        barrier = pltpu.get_barrier_semaphore()

        @pl.loop(1, owners)
        def _(i):
            pl.semaphore_signal(
                barrier, inc=1, device_id=coords(lax.rem(me + i, owners)), device_id_type=pl.DeviceIdType.MESH
            )

        pl.semaphore_wait(barrier, owners - 1)

        @pl.loop(0, x_ref.shape[0])
        def _(step):
            own(step).start()

            @pl.loop(1, owners)
            def _(i):
                remote(step, i).start()

    own(q).wait()

    others = recv.at[q, pl.ds(0, owners - 1)]
    pltpu.make_async_copy(others, others, recv_sem.at[q]).wait()

    @pl.when(q == count - 1)
    def _():
        @pl.loop(0, x_ref.shape[0])
        def _(step):
            gone = recv.at[step, pl.ds(0, owners - 1)]
            pltpu.make_async_copy(gone, gone, send_sem.at[step]).wait()

    for g in range(total_segs):
        c, s = g // segs, g % segs
        x = jnp.concatenate(
            [
                recv[q, st * blocks + c, (p * segs + s) * local_rows : (p * segs + s + 1) * local_rows, :]
                for p in range(2)
                for st in range(groups)
            ],
            axis=0,
        )
        t = dot(x, sel_ref[...], ((0,), (0,)))
        wide[pl.ds(2 * g * ROOT, ROOT), :] = t[:, :128]
        wide[pl.ds((2 * g + 1) * ROOT, ROOT), :] = t[:, 128:]
    a = lax.broadcasted_iota(jnp.int32, (S, 128), 0)
    lane = lax.broadcasted_iota(jnp.int32, (S, 128), 1)
    straight = jnp.where(lane < S, lane - a, a - lane + S - 1) >= 0
    left = lax.broadcasted_iota(jnp.int32, (8, 128), 1) < S

    @pl.loop(0, ROOT // 8)
    def _(block):
        for c in range(8):
            w = wide[pl.ds(block * 8 + c, 2 * total_segs, stride=ROOT), :].astype(BF16)
            out = dot(w[:, :S], w, ((0,), (0,))) * (1.0 / total_segs)
            packed[c * S : (c + 1) * S, :] = jnp.where(straight, out, pltpu.roll(out, S, 1))
        for j in range(S // 2):
            even = packed[pl.ds(2 * j, 8, stride=S), :]
            odd = packed[pl.ds(2 * j + 1, 8, stride=S), :]
            o_ref[pl.ds(pl.multiple_of(block * 8, 8), 8), j * 128 : (j + 1) * 128] = jnp.where(left, even, odd)


def cross(x, sel, groups, blocks, segs, local_rows):
    owned = x.shape[0]
    total_segs = blocks * segs
    return pl.pallas_call(
        functools.partial(cross_kernel, groups, blocks, segs, local_rows),
        grid=(owned,),
        in_specs=[
            pl.BlockSpec(memory_space=pl.ANY),
            pl.BlockSpec((2 * S, 4 * S), lambda q: (0, 0)),
        ],
        out_specs=pl.BlockSpec((ROOT, S * S), lambda q: (q, 0)),
        out_shape=jax.ShapeDtypeStruct((owned * ROOT, S * S), F32),
        scratch_shapes=[
            pltpu.VMEM(x.shape, BF16),
            pltpu.VMEM((2 * total_segs * ROOT, 128), F32),
            pltpu.VMEM((8 * S, 128), F32),
            pltpu.SemaphoreType.DMA((owned,)),
            pltpu.SemaphoreType.DMA((owned,)),
            pltpu.SemaphoreType.DMA((owned,)),
        ],
        compiler_params=pltpu.CompilerParams(
            vmem_limit_bytes=48 * 1024 * 1024, collective_id=0, has_side_effects=True
        ),
        name="cross",
    )(x, sel)


def shards(samples, delays, fringe_rate, station_of_row):
    _, local_rows, local_time = samples.shape
    segs = local_time // NCH
    groups = lax.axis_size("station")
    blocks = lax.axis_size("cores")
    owners = groups * blocks
    head = samples[:, :, :MAXD].reshape(2, local_rows, MAXD // ROOT, ROOT)
    following = passed_along(head, "cores", -1)
    shaped = samples.reshape(2, local_rows, local_time // ROOT, ROOT)
    index = jnp.arange(ROOT, dtype=jnp.int32)
    u = phases(fringe_rate[:, None] * (ROOT * index)[None, :])
    start = (lax.axis_index("cores") * segs + jnp.arange(segs, dtype=jnp.int32)) * NCH % PERIOD
    v = phases(fringe_rate[:, None, None] * (start[:, None] + index[None, :])[None])
    spectra = front(shaped, following, delays, u, v, owners)
    owned = spectra.shape[4]
    sent = spectra.transpose(4, 0, 1, 2, 3, 5).reshape(owned, owners, 2 * segs * local_rows, ROOT)
    pick = (station_of_row[:, None] == jnp.arange(S, dtype=jnp.int32)[None, :]).astype(BF16)
    none = jnp.zeros_like(pick)
    sel = jnp.concatenate(
        [
            jnp.concatenate([pick, none, none, pick], axis=1),
            jnp.concatenate([none, -pick, pick, none], axis=1),
        ],
        axis=0,
    )
    return cross(sent, sel, groups, blocks, segs, local_rows)


def solution(mesh):
    in_specs = (P(None, "station", "cores"), P("station"), P("station"), P())
    out_specs = P(("station", "cores"), None)
    return jax.shard_map(shards, mesh=mesh, in_specs=in_specs, out_specs=out_specs, check_vma=False)
```

```python
import functools
import math

import jax
import jax.numpy as jnp
import numpy as np
from jax import lax
from jax.experimental import pallas as pl
from jax.experimental.pallas import tpu as pltpu
from jax.sharding import PartitionSpec as P

S = 64
NCH = 65536
ROOT = 256
MAXD = 32768
PERIOD = 262144
F32 = jnp.float32
BF16 = jnp.bfloat16


def passed_along(x, axis, by):
    count = lax.axis_size(axis)
    pairs = [(i, i + by) for i in range(count) if 0 <= i + by < count]
    return lax.ppermute(x, axis, pairs)


def dft_table(length, scale):
    index = np.arange(ROOT)
    angle = (index[:, None] * index[None, :] % length) * (2.0 * math.pi / length)
    return np.stack([np.cos(angle) * scale, -np.sin(angle) * scale]).astype(np.float32)


def halves(x):
    high = x.astype(BF16)
    return high, (x - high.astype(F32)).astype(BF16)


def block_form(real, imag):
    return jnp.concatenate(
        [jnp.concatenate([real, -imag], axis=1), jnp.concatenate([imag, real], axis=1)], axis=0
    )


def dot(a, b, dims=((1,), (0,))):
    return lax.dot_general(a, b, (dims, ((), ())), preferred_element_type=F32)


def phases(counter):
    angle = (counter % PERIOD).astype(F32) * (2.0 * math.pi / PERIOD)
    return jnp.stack([jnp.cos(angle), -jnp.sin(angle)], axis=-2)


def front_kernel(segs, delays, x_ref, follow_ref, u_ref, v_ref, f_ref, tw_ref, gh_ref, gl_ref, o_ref, ext):
    r = pl.program_id(0)
    here = x_ref.shape[2]
    after = follow_ref.shape[2]
    for p in range(2):
        for h in range(2):
            cols = slice(h * 128, h * 128 + 128)
            ext[p, h, :here] = x_ref[p, 0, :, cols].astype(F32)
            ext[p, h, here : here + after] = follow_ref[p, 0, :, cols].astype(F32)
    delay = delays[r]
    down = delay // ROOT
    across = delay % ROOT
    u_real, u_imag = u_ref[0, 0:1], u_ref[0, 1:2]
    f_real, f_imag = f_ref[0], f_ref[1]
    fh_real, fl_real = halves(f_real * u_real - f_imag * u_imag)
    fh_imag, fl_imag = halves(f_real * u_imag + f_imag * u_real)
    f_high = block_form(fh_real, fh_imag)
    f_low = block_form(fl_real, fl_imag)
    lane = lax.broadcasted_iota(jnp.int32, (ROOT, ROOT), 1)
    kept = lane >= across
    for s in range(segs):
        parts = []
        for p in range(2):
            begin = down + s * ROOT
            first = jnp.concatenate([ext[p, h, pl.ds(begin, ROOT), :] for h in range(2)], axis=1)
            second = jnp.concatenate([ext[p, h, pl.ds(begin + 1, ROOT), :] for h in range(2)], axis=1)
            parts.append(pltpu.roll(jnp.where(kept, first, second), ROOT - across, 1).astype(BF16))
        x = jnp.concatenate(parts, axis=0)
        y = dot(f_high, x) + dot(f_low, x)
        y_real, y_imag = y[:ROOT], y[ROOT:]
        v_real, v_imag = v_ref[0, s, 0:1], v_ref[0, s, 1:2]
        t_real = tw_ref[0] * v_real - tw_ref[1] * v_imag
        t_imag = tw_ref[0] * v_imag + tw_ref[1] * v_real
        mh_real, ml_real = halves(y_real * t_real - y_imag * t_imag)
        mh_imag, ml_imag = halves(y_real * t_imag + y_imag * t_real)
        high = jnp.concatenate([mh_real, mh_imag], axis=1)
        low = jnp.concatenate([ml_real, ml_imag], axis=1)
        rows = ((1,), (1,))
        z = dot(gh_ref[...], high, rows) + dot(gh_ref[...], low, rows) + dot(gl_ref[...], high, rows)
        z = z.astype(BF16)
        for p in range(2):
            o_ref[:, p, s, 0] = z[p * ROOT : (p + 1) * ROOT].reshape(o_ref.shape[0], o_ref.shape[4], ROOT)


def front(samples, following, delays, u, v, owners):
    _, local_rows, here, _ = samples.shape
    after = following.shape[2]
    segs = here // ROOT
    owned = ROOT // owners
    table = dft_table(ROOT, 1.0)
    gh, gl = halves(block_form(jnp.asarray(table[0]), jnp.asarray(table[1])))
    whole3 = pl.BlockSpec((2, ROOT, ROOT), lambda r, d: (0, 0, 0))
    whole2 = pl.BlockSpec((2 * ROOT, 2 * ROOT), lambda r, d: (0, 0))
    return pl.pallas_call(
        functools.partial(front_kernel, segs),
        grid_spec=pltpu.PrefetchScalarGridSpec(
            num_scalar_prefetch=1,
            grid=(local_rows,),
            in_specs=[
                pl.BlockSpec((2, 1, here, ROOT), lambda r, d: (0, r, 0, 0)),
                pl.BlockSpec((2, 1, after, ROOT), lambda r, d: (0, r, 0, 0)),
                pl.BlockSpec((1, 2, ROOT), lambda r, d: (r, 0, 0)),
                pl.BlockSpec((1, segs, 2, ROOT), lambda r, d: (r, 0, 0, 0)),
                whole3,
                whole3,
                whole2,
                whole2,
            ],
            out_specs=pl.BlockSpec((owners, 2, segs, 1, owned, ROOT), lambda r, d: (0, 0, 0, r, 0, 0)),
            scratch_shapes=[
                pltpu.VMEM((2, 2, here + after + 8, 128), F32),
            ],
        ),
        out_shape=jax.ShapeDtypeStruct((owners, 2, segs, local_rows, owned, ROOT), BF16),
        compiler_params=pltpu.CompilerParams(vmem_limit_bytes=56 * 1024 * 1024),
        name="front",
    )(delays, samples, following, u, v, jnp.asarray(table), jnp.asarray(dft_table(NCH, 1.0 / 256.0)), gh, gl)


def products(groups, blocks, segs, local_rows, arrived, sel_ref, o_ref, wide, packed):
    total_segs = blocks * segs
    for g in range(total_segs):
        c, s = g // segs, g % segs
        x = jnp.concatenate(
            [
                arrived[st * blocks + c, (p * segs + s) * local_rows : (p * segs + s + 1) * local_rows, :]
                for p in range(2)
                for st in range(groups)
            ],
            axis=0,
        )
        t = dot(x, sel_ref[...], ((0,), (0,)))
        wide[pl.ds(2 * g * ROOT, ROOT), :] = t[:, :128]
        wide[pl.ds((2 * g + 1) * ROOT, ROOT), :] = t[:, 128:]
    a = lax.broadcasted_iota(jnp.int32, (S, 128), 0)
    lane = lax.broadcasted_iota(jnp.int32, (S, 128), 1)
    straight = jnp.where(lane < S, lane - a, a - lane + S - 1) >= 0
    left = lax.broadcasted_iota(jnp.int32, (8, 128), 1) < S

    @pl.loop(0, ROOT // 8)
    def _(block):
        for c in range(8):
            w = wide[pl.ds(block * 8 + c, 2 * total_segs, stride=ROOT), :].astype(BF16)
            out = dot(w[:, :S], w, ((0,), (0,))) * (1.0 / total_segs)
            packed[c * S : (c + 1) * S, :] = jnp.where(straight, out, pltpu.roll(out, S, 1))
        for j in range(S // 2):
            even = packed[pl.ds(2 * j, 8, stride=S), :]
            odd = packed[pl.ds(2 * j + 1, 8, stride=S), :]
            o_ref[pl.ds(pl.multiple_of(block * 8, 8), 8), j * 128 : (j + 1) * 128] = jnp.where(left, even, odd)


def cross_kernel(groups, blocks, segs, local_rows, x_ref, sel_ref, o_ref, last_ref, recv, wide, packed, send_sem, recv_sem, own_sem):
    q = pl.program_id(0)
    count = pl.num_programs(0)
    owners = groups * blocks
    me = lax.axis_index("station") * blocks + lax.axis_index("cores")

    def coords(d):
        return {"station": d // blocks, "cores": lax.rem(d, blocks)}

    def remote(step, i):
        dest = lax.rem(me + i, owners)
        return pltpu.make_async_remote_copy(
            src_ref=x_ref.at[step, dest],
            dst_ref=recv.at[step, me],
            send_sem=send_sem.at[step],
            recv_sem=recv_sem.at[step],
            device_id=coords(dest),
            device_id_type=pl.DeviceIdType.MESH,
        )

    def own(step):
        return pltpu.make_async_copy(x_ref.at[step, me], recv.at[step, me], own_sem.at[step])

    @pl.when(q == 0)
    def _():
        barrier = pltpu.get_barrier_semaphore()

        @pl.loop(1, owners)
        def _(i):
            pl.semaphore_signal(
                barrier, inc=1, device_id=coords(lax.rem(me + i, owners)), device_id_type=pl.DeviceIdType.MESH
            )

        pl.semaphore_wait(barrier, owners - 1)

        @pl.loop(0, x_ref.shape[0])
        def _(step):
            own(step).start()

            @pl.loop(1, owners)
            def _(i):
                remote(step, i).start()

    own(q).wait()

    others = recv.at[q, pl.ds(0, owners - 1)]
    pltpu.make_async_copy(others, others, recv_sem.at[q]).wait()

    @pl.when(q == count - 1)
    def _():
        @pl.loop(0, x_ref.shape[0])
        def _(step):
            gone = recv.at[step, pl.ds(0, owners - 1)]
            pltpu.make_async_copy(gone, gone, send_sem.at[step]).wait()

    @pl.when(q < count - 1)
    def _():
        products(groups, blocks, segs, local_rows, recv.at[q], sel_ref, o_ref, wide, packed)

    @pl.when(q == count - 1)
    def _():
        pltpu.sync_copy(recv.at[q], last_ref)


def last_kernel(groups, blocks, segs, local_rows, x_ref, sel_ref, done_ref, o_ref, tile, wide, packed, sems, tile_sem):
    count = done_ref.shape[0] // ROOT

    def moved(step):
        rows = pl.ds(step * ROOT, ROOT)
        return pltpu.make_async_copy(done_ref.at[rows], o_ref.at[rows], sems.at[step])

    for step in range(count):
        moved(step).start()
    products(groups, blocks, segs, local_rows, x_ref, sel_ref, tile, wide, packed)
    final = pltpu.make_async_copy(tile, o_ref.at[pl.ds(count * ROOT, ROOT)], tile_sem)
    final.start()
    for step in range(count):
        moved(step).wait()
    final.wait()


def cross(x, sel, groups, blocks, segs, local_rows):
    owned = x.shape[0]
    total_segs = blocks * segs
    done, last = pl.pallas_call(
        functools.partial(cross_kernel, groups, blocks, segs, local_rows),
        grid=(owned,),
        in_specs=[
            pl.BlockSpec(memory_space=pl.ANY),
            pl.BlockSpec((2 * S, 4 * S), lambda q: (0, 0)),
        ],
        out_specs=[
            pl.BlockSpec((ROOT, S * S), lambda q: (jnp.minimum(q, owned - 2), 0)),
            pl.BlockSpec(memory_space=pl.ANY),
        ],
        out_shape=[
            jax.ShapeDtypeStruct(((owned - 1) * ROOT, S * S), F32),
            jax.ShapeDtypeStruct(x.shape[1:], BF16),
        ],
        scratch_shapes=[
            pltpu.VMEM(x.shape, BF16),
            pltpu.VMEM((2 * total_segs * ROOT, 128), F32),
            pltpu.VMEM((8 * S, 128), F32),
            pltpu.SemaphoreType.DMA((owned,)),
            pltpu.SemaphoreType.DMA((owned,)),
            pltpu.SemaphoreType.DMA((owned,)),
        ],
        compiler_params=pltpu.CompilerParams(
            vmem_limit_bytes=48 * 1024 * 1024, collective_id=0, has_side_effects=True
        ),
        name="cross",
    )(x, sel)
    return pl.pallas_call(
        functools.partial(last_kernel, groups, blocks, segs, local_rows),
        in_specs=[
            pl.BlockSpec(memory_space=pltpu.VMEM),
            pl.BlockSpec(memory_space=pltpu.VMEM),
            pl.BlockSpec(memory_space=pl.ANY),
        ],
        out_specs=pl.BlockSpec(memory_space=pl.ANY),
        out_shape=jax.ShapeDtypeStruct((owned * ROOT, S * S), F32),
        scratch_shapes=[
            pltpu.VMEM((ROOT, S * S), F32),
            pltpu.VMEM((2 * total_segs * ROOT, 128), F32),
            pltpu.VMEM((8 * S, 128), F32),
            pltpu.SemaphoreType.DMA((owned - 1,)),
            pltpu.SemaphoreType.DMA,
        ],
        compiler_params=pltpu.CompilerParams(vmem_limit_bytes=48 * 1024 * 1024),
        name="last",
    )(last, sel, done)


def shards(samples, delays, fringe_rate, station_of_row):
    _, local_rows, local_time = samples.shape
    segs = local_time // NCH
    groups = lax.axis_size("station")
    blocks = lax.axis_size("cores")
    owners = groups * blocks
    head = samples[:, :, :MAXD].reshape(2, local_rows, MAXD // ROOT, ROOT)
    following = passed_along(head, "cores", -1)
    shaped = samples.reshape(2, local_rows, local_time // ROOT, ROOT)
    index = jnp.arange(ROOT, dtype=jnp.int32)
    u = phases(fringe_rate[:, None] * (ROOT * index)[None, :])
    start = (lax.axis_index("cores") * segs + jnp.arange(segs, dtype=jnp.int32)) * NCH % PERIOD
    v = phases(fringe_rate[:, None, None] * (start[:, None] + index[None, :])[None])
    spectra = front(shaped, following, delays, u, v, owners)
    owned = spectra.shape[4]
    sent = spectra.transpose(4, 0, 1, 2, 3, 5).reshape(owned, owners, 2 * segs * local_rows, ROOT)
    pick = (station_of_row[:, None] == jnp.arange(S, dtype=jnp.int32)[None, :]).astype(BF16)
    none = jnp.zeros_like(pick)
    sel = jnp.concatenate(
        [
            jnp.concatenate([pick, none, none, pick], axis=1),
            jnp.concatenate([none, -pick, pick, none], axis=1),
        ],
        axis=0,
    )
    return cross(sent, sel, groups, blocks, segs, local_rows)


def solution(mesh):
    in_specs = (P(None, "station", "cores"), P("station"), P("station"), P())
    out_specs = P(("station", "cores"), None)
    return jax.shard_map(shards, mesh=mesh, in_specs=in_specs, out_specs=out_specs, check_vma=False)
```
